256 devices in a mesh: ctx: 32 (over z, x_hi, core), head: 8 (over x_lo, y).
Axes of the slice: x: 4 (x_hi: 2, x_lo: 2; x = x_hi * 2 + x_lo), y: 4, z: 8, core: 2. Of those that a mesh axis runs over, the one named last changes fastest.
Arguments:
- queries: bfloat16 [16384, 64, 128], P('ctx', 'head'), may hold values from -160 to 160, as said below
- keys: bfloat16 [16384, 8, 128], P('ctx', 'head'), may hold values from -4 to 4
- values: bfloat16 [16384, 8, 128], P('ctx', 'head'), may hold values from -6 to 6
- doc_lengths: int32 [64], replicated, may hold values from 1 to 4096, 16384 in all
Outputs:
- attended: bfloat16 [16384, 8192], P(('ctx', 'head'))
The draws below stay inside these ranges and needn't reach their ends.
Inputs may be any that keep to these rules, and one draw needn't show every extreme that they name: `queries`: queries of several heads for a few tokens may be large multiples of sums of earlier keys of the same key head. `doc_lengths`: the lengths sum to 16384; the largest is exactly 4096.
All inputs are finite; a program needn't handle non-finite values.
Results may differ from the reference program's by a relative error of at most 0.0033.
Values may be sent and summed in bfloat16 or wider, within the bound.
No kernel may reach another device: no remote copies, remote signals or barrier semaphores. Data moves between devices by JAX's collectives and lax.ppermute only.
A program may use at most 64 MiB of HBM per device.

```python
import math
import jax
import jax.numpy as jnp
import numpy as np
from jax import lax

HD = 128
TOK_DEV = 512
SPAN = 8
KV_HEADS = 8
QH = 64
TOKENS = 16384
DOCS = 64
DOC_MOST = 4096


def make_pair(key):
    key_keys = jax.random.fold_in(key, 11)
    key_queries = jax.random.fold_in(key, 23)
    key_vectors = jnp.clip(jax.random.normal(key_keys, (TOKENS, KV_HEADS, HD), jnp.float32), -4.0, 4.0)
    query_vectors = jnp.clip(jax.random.normal(key_queries, (TOKENS, QH, HD), jnp.float32), -6.0, 6.0)
    return (query_vectors, key_vectors)


def draw_queries(key, part):
    return make_pair(key)[0].astype(jnp.bfloat16)


def draw_keys(key, part):
    return make_pair(key)[1].astype(jnp.bfloat16)


def shard_levels(key, extent, shards, least, high):
    def one(dim, parts):
        heights = jax.random.uniform(jax.random.fold_in(jax.random.fold_in(key, 6), dim), (parts,), jnp.float32, least / len(shards), high / len(shards))
        return jnp.repeat(jnp.exp(heights), extent[dim] // parts).reshape((-1,) + (1,) * (len(extent) - dim - 1))

    gain = one(*shards[0])
    for cut in shards[1:]:
        gain = gain * one(*cut)
    return gain


def split_up(number_of, total, bound, lean):
    portions = [(1 << 20) // math.isqrt(grade ** lean) + 1 for grade in range(2, number_of + 1)]
    rest, counts = total - bound - (number_of - 1), [1] * (number_of - 1)
    while rest > 0:
        candidates = [i for i in range(number_of - 1) if counts[i] < bound]
        pool, left = sum([portions[i] for i in candidates]), rest
        for i in candidates:
            extra = min(bound - counts[i], max(1, left * portions[i] // pool), rest)
            counts[i] = counts[i] + extra
            rest = rest - extra
    return np.array([bound] + counts)


def ragged_sizes(rng, amount, total, limit, slope):
    if amount == 2:
        one = jax.random.randint(rng, (), max(1, total - limit), min(limit, total - 1) + 1)
        return jnp.stack([one, total - one])
    tallies = jnp.asarray(split_up(amount, total, limit, slope), jnp.int32)
    pairs = (amount - 1) // 2
    source_of, receiver = tallies[1:1 + 2 * pairs:2], tallies[2:2 + 2 * pairs:2]
    slack = jnp.minimum(source_of - 1, limit - receiver)
    passed = jax.random.randint(jax.random.fold_in(rng, 1), (pairs,), 0, 1 << 20) % (slack + 1)
    tallies = tallies.at[1:1 + 2 * pairs:2].set(source_of - passed).at[2:2 + 2 * pairs:2].set(receiver + passed)
    return tallies[jax.random.permutation(jax.random.fold_in(rng, 2), amount)]


def noise(key, extent, width, most, shards=(), kind=jnp.bfloat16):
    level = shard_levels(key, extent, shards, -0.22, 0.18) if shards else 1.0
    values = jax.random.normal(key, extent, jnp.float32) * width * level
    return jnp.minimum(jnp.maximum(values, -most), most).astype(kind)


def setup_inputs(seed: int = 0) -> dict:
    arg_keys = jax.random.split(jax.random.key(seed), 5)
    queries = draw_queries(jax.random.fold_in(arg_keys[4], 71), 0)
    keys = draw_keys(jax.random.fold_in(arg_keys[4], 71), 0)
    values = noise(arg_keys[2], (TOKENS, KV_HEADS, HD), 1.0, 6.0, ((0, 32), (1, 8)))
    doc_lengths = ragged_sizes(arg_keys[3], DOCS, TOKENS, DOC_MOST, 2).astype(jnp.int32)
    return {"queries": queries, "keys": keys, "values": values, "doc_lengths": doc_lengths}


def doc_index(positions, ends):
    return jnp.sum((ends[None, :] <= positions[:, None]).astype(jnp.int32), axis=1).astype(jnp.int32)


def reference(queries, keys, values, doc_lengths):
    tokens, qheads, hdim = queries.shape
    kvheads = keys.shape[1]
    group = qheads // kvheads
    block = TOK_DEV
    scale = 1.0 / (hdim ** 0.5)
    ends = jnp.cumsum(doc_lengths).astype(jnp.int32)
    docs = doc_index(jnp.arange(tokens, dtype=jnp.int32), ends)
    front = jnp.zeros((SPAN * block, kvheads, hdim), keys.dtype)
    key_pad = jnp.concatenate([front, keys], axis=0)
    value_pad = jnp.concatenate([front, values], axis=0)
    grouped = queries.reshape(tokens, kvheads, group, hdim)

    def one_block(index):
        start = (index * block).astype(jnp.int32)
        query_block = lax.dynamic_slice_in_dim(grouped, start, block, 0).astype(jnp.float32)
        qpos = start + jnp.arange(block, dtype=jnp.int32)
        qdoc = lax.dynamic_slice_in_dim(docs, start, block, 0)

        def update(state, back):
            first = (start - back * block).astype(jnp.int32)
            key_block = lax.dynamic_slice_in_dim(key_pad, first + SPAN * block, block, 0).astype(jnp.float32)
            value_block = lax.dynamic_slice_in_dim(value_pad, first + SPAN * block, block, 0).astype(jnp.float32)
            kpos = first + jnp.arange(block, dtype=jnp.int32)
            kdoc = doc_index(jnp.maximum(kpos, 0), ends)
            mask = (kdoc[None, :] == qdoc[:, None]) & (kpos[None, :] <= qpos[:, None]) & (kpos[None, :] >= 0)
            highest, total, acc = state
            score = jnp.einsum("qhgd,khd->hgqk", query_block, key_block) * scale
            score = jnp.where(mask[None, None], score, -1e30)
            newmax = jnp.maximum(highest, jnp.max(score, axis=-1))
            factor = jnp.exp(highest - newmax)
            expo = jnp.exp(score - newmax[..., None])
            total = total * factor + jnp.sum(expo, axis=-1)
            rounded = lax.optimization_barrier(expo.astype(jnp.bfloat16)).astype(jnp.float32)
            acc = acc * factor[..., None] + jnp.einsum("hgqk,khd->hgqd", rounded, value_block)
            return newmax, total, acc

        def step(back, state):
            first = (start - back * block).astype(jnp.int32)
            last = first + block - 1
            need = (back == 0) | ((last >= 0) & (doc_index(jnp.maximum(last, 0)[None], ends)[0] == qdoc[0]))
            return lax.cond(need, lambda s: update(s, back), lambda s: s, state)

        init = (jnp.full((kvheads, group, block), -1e30, jnp.float32),
                jnp.zeros((kvheads, group, block), jnp.float32),
                jnp.zeros((kvheads, group, block, hdim), jnp.float32))
        highest, total, acc = lax.fori_loop(0, SPAN + 1, step, init)
        result = acc / total[..., None]
        return jnp.transpose(result, (2, 0, 1, 3)).reshape(block, qheads * hdim).astype(jnp.bfloat16)

    outs = lax.map(one_block, jnp.arange(tokens // block, dtype=jnp.int32))
    return outs.reshape(tokens, qheads * hdim)
```

```python
import functools

import jax
import jax.numpy as jnp
from jax import lax
from jax.experimental import pallas as pl
from jax.experimental.pallas import tpu as pltpu
from jax.sharding import PartitionSpec as P

NEG = -1e30
NT = (((1,), (1,)), ((), ()))
FAR = ((0, 1), (0, 2), (0, 3), (1, 0), (1, 1), (1, 2), (1, 3), (2, 0), (2, 1), (2, 2), (2, 3))


def kernel(rows, group, tile, sub, factor, me_ref, len_ref, q_ref, *refs):
    count = len(FAR) + 1
    kv_in, out_ref = refs[:count], refs[count]
    kv, m_s, l_s, a_s, start_s, sems = refs[count + 1 :]
    copies = [pltpu.make_async_copy(kv_in[b], kv.at[b], sems.at[b]) for b in range(count)]
    for c in copies:
        c.start()
    me = me_ref[0]
    base = me * rows
    tokens = lax.broadcasted_iota(jnp.int32, (rows, 128), 0)
    ntiles = rows // tile
    start_s[...] = jnp.zeros_like(start_s)

    def doc(d, carry):
        end, lows, highs = carry
        end = end + len_ref[d]
        lows = tuple(jnp.where(end <= base + i * tile, end, lows[i]) for i in range(ntiles))
        highs = tuple(jnp.where(end <= base + i * tile + tile - 1, end, highs[i]) for i in range(ntiles))

        @pl.when(end < base + rows)
        def _():
            @pl.when((end > base) | (end + len_ref[jnp.minimum(d + 1, len_ref.shape[0] - 1)] > base))
            def _():
                start_s[...] = jnp.where(tokens + base >= end, end, start_s[...])

        return end, lows, highs

    zeros = (jnp.int32(0),) * ntiles
    _, lows, highs = lax.fori_loop(0, len_ref.shape[0], doc, (jnp.int32(0), zeros, zeros))
    m_s[...] = jnp.full_like(m_s, NEG)
    l_s[...] = jnp.zeros_like(l_s)
    a_s[...] = jnp.zeros_like(a_s)
    for c in copies:
        c.wait()
    lane = lax.broadcasted_iota(jnp.int32, (1, 128), 1)

    def update(b, first, r, n, k0, keys, masked, causal):
        rs = pl.ds(r, n)
        s = lax.dot_general(q_ref[rs, :], kv[b, k0 : k0 + keys, 0:128], NT, preferred_element_type=jnp.float32)
        parts = [s[:, 128 * j : 128 * j + 128] for j in range(keys // 128)]
        if masked:
            t0, nt = r // group, n // group
            spread = lambda x: jnp.broadcast_to(x[:, None, :], (nt, group, 128)).reshape(n, 128)
            low = spread(start_s[pl.ds(t0, nt), :])
            if causal:
                high = spread(base + t0 + lax.broadcasted_iota(jnp.int32, (nt, 128), 0))
            for j in range(len(parts)):
                pos = first + k0 + 128 * j + lane
                ok = pos >= low
                if causal:
                    ok = ok & (pos <= high)
                parts[j] = jnp.where(ok, parts[j], NEG)
        m = m_s[rs, :]
        top = jnp.max(functools.reduce(jnp.maximum, parts), axis=1, keepdims=True)
        new = jnp.maximum(m, jnp.broadcast_to(top, m.shape))
        parts = [jnp.exp2((x - new) * factor) for x in parts]
        scale = jnp.exp2((m - new) * factor)
        weight = jnp.concatenate([x.astype(jnp.bfloat16) for x in parts], axis=1)
        m_s[rs, :] = new
        l_s[rs, :] = l_s[rs, :] * scale + functools.reduce(jnp.add, parts)
        a_s[rs, :] = a_s[rs, :] * scale + jnp.dot(
            weight, kv[b, k0 : k0 + keys, 128:256], preferred_element_type=jnp.float32
        )

    step = 128
    for t in range(0, rows, step):
        update(0, base, t * group, step * group, 0, t + step, True, True)
    for i in range(ntiles):
        low, high = lows[i], highs[i]

        def block(b, _):
            index = lax.bitwise_xor(me - 4 * (b >> 2), b & 3)
            first = index * rows

            @pl.when((index >= 0) & (index < me) & (first + rows > low))
            def _():
                @pl.when(high <= first)
                def _():
                    for r in range(0, tile * group, sub):
                        update(b, first, i * tile * group + r, sub, 0, rows, False, False)

                @pl.when(high > first)
                def _():
                    for r in range(0, tile * group, sub):
                        update(b, first, i * tile * group + r, sub, 0, rows, True, False)

            return 0

        lax.fori_loop(1, count, block, 0)
    total = jnp.sum(l_s[...], axis=1, keepdims=True)
    out_ref[...] = (a_s[...] / total).astype(out_ref.dtype)


def attend(me, doc_lengths, q, blocks, rows, group, tile=256, sub=2048):
    n, hdim = q.shape
    factor = 1.4426950408889634 / hdim**0.5
    vmem = pl.BlockSpec(memory_space=pltpu.VMEM)
    smem = pl.BlockSpec(memory_space=pltpu.SMEM)
    return pl.pallas_call(
        functools.partial(kernel, rows, group, tile, sub, factor),
        out_shape=jax.ShapeDtypeStruct((n, hdim), jnp.bfloat16),
        in_specs=[smem, smem, vmem] + [pl.BlockSpec(memory_space=pl.ANY)] * len(blocks),
        out_specs=vmem,
        scratch_shapes=[
            pltpu.VMEM((len(blocks), rows, 2 * hdim), jnp.bfloat16),
            pltpu.VMEM((n, hdim), jnp.float32),
            pltpu.VMEM((n, hdim), jnp.float32),
            pltpu.VMEM((n, hdim), jnp.float32),
            pltpu.VMEM((rows, hdim), jnp.int32),
            pltpu.SemaphoreType.DMA((len(blocks),)),
        ],
        compiler_params=pltpu.CompilerParams(vmem_limit_bytes=40 << 20),
        cost_estimate=pl.CostEstimate(flops=20_000_000_000, bytes_accessed=6_000_000, transcendentals=19_000_000),
    )(me, doc_lengths, q, *blocks)


def on_device(queries, keys, values, doc_lengths):
    rows, group, hdim = queries.shape
    count = lax.axis_size("ctx")
    heads = lax.axis_size("head")
    me = lax.axis_index("ctx").reshape(1)
    own = jnp.concatenate([keys[:, 0, :], values[:, 0, :]], axis=1)

    def swap(x, bit):
        return lax.ppermute(x, "ctx", [(i, i ^ bit) for i in range(count)])

    def plane(x):
        return lax.ppermute(x, "ctx", [(i, i + 4) for i in range(count - 4)])

    z1 = plane(own)
    x0 = swap(own, 2)
    c0 = swap(own, 1)
    z2 = plane(z1)
    x1 = swap(z1, 2)
    xc0 = swap(x0, 1)
    c1 = swap(z1, 1)
    x2 = lax.ppermute(z2, "ctx", [(i, i ^ 2) for i in range(count) if i & 2])
    xc1 = swap(x1, 1)
    c2 = swap(z2, 1)
    xc2 = swap(x2, 1)
    blocks = [own, c0, x0, xc0, z1, c1, x1, xc1, z2, c2, x2, xc2]
    out = attend(me, doc_lengths, queries.reshape(rows * group, hdim), blocks, rows, group)
    out = lax.all_to_all(out.reshape(heads, -1, hdim), "head", split_axis=0, concat_axis=0, tiled=True)
    out = out.reshape(heads, rows // heads, group, hdim)
    return jnp.transpose(out, (1, 0, 2, 3)).reshape(rows // heads, heads * group * hdim)


def solution(mesh):
    placed = (P("ctx", "head", None), P("ctx", "head", None), P("ctx", "head", None), P())
    return jax.shard_map(
        on_device, mesh=mesh, in_specs=placed, out_specs=P(("ctx", "head"), None), check_vma=False
    )
```

```python
import functools

import jax
import jax.numpy as jnp
from jax import lax
from jax.experimental import pallas as pl
from jax.experimental.pallas import tpu as pltpu
from jax.sharding import PartitionSpec as P

NEG = -1e30
NT = (((1,), (1,)), ((), ()))


def kernel(first_stage, last_stage, origin, rows, group, tile, sub, factor, me_ref, len_ref, q_ref, *refs):
    refs, sems = refs[:-1], refs[-1]
    refs, kv, start_s = refs[:-2], refs[-2], refs[-1]
    count = kv.shape[0]
    kv_in, refs = refs[:count], refs[count:]
    copies = [pltpu.make_async_copy(kv_in[b], kv.at[b], sems.at[b]) for b in range(count)]
    for c in copies:
        c.start()
    if not first_stage:
        refs = refs[3:]
    m_s, l_s, a_s = refs[-3:]
    me = me_ref[0]
    base = me * rows
    tokens = lax.broadcasted_iota(jnp.int32, (rows, 128), 0)
    ntiles = rows // tile
    start_s[...] = jnp.zeros_like(start_s)

    def doc(d, carry):
        end, lows, highs = carry
        end = end + len_ref[d]
        lows = tuple(jnp.where(end <= base + i * tile, end, lows[i]) for i in range(ntiles))
        highs = tuple(jnp.where(end <= base + i * tile + tile - 1, end, highs[i]) for i in range(ntiles))

        @pl.when(end < base + rows)
        def _():
            @pl.when(end + len_ref[jnp.minimum(d + 1, len_ref.shape[0] - 1)] > base)
            def _():
                start_s[...] = jnp.where(tokens + base >= end, end, start_s[...])

        return end, lows, highs

    zeros = (jnp.int32(0),) * ntiles
    _, lows, highs = lax.fori_loop(0, len_ref.shape[0], doc, (jnp.int32(0), zeros, zeros))
    if first_stage:
        m_s[...] = jnp.full_like(m_s, NEG)
        l_s[...] = jnp.zeros_like(l_s)
        a_s[...] = jnp.zeros_like(a_s)
    for c in copies:
        c.wait()
    lane = lax.broadcasted_iota(jnp.int32, (1, 128), 1)

    def update(b, first, r, n, k0, keys, masked, causal):
        rs = pl.ds(r, n)
        s = lax.dot_general(q_ref[rs, :], kv[b, k0 : k0 + keys, 0:128], NT, preferred_element_type=jnp.float32)
        parts = [s[:, 128 * j : 128 * j + 128] for j in range(keys // 128)]
        if masked:
            t0, nt = r // group, n // group
            spread = lambda x: jnp.broadcast_to(x[:, None, :], (nt, group, 128)).reshape(n, 128)
            low = spread(start_s[pl.ds(t0, nt), :])
            if causal:
                high = spread(base + t0 + lax.broadcasted_iota(jnp.int32, (nt, 128), 0))
            for j in range(len(parts)):
                pos = first + k0 + 128 * j + lane
                ok = pos >= low
                if causal:
                    ok = ok & (pos <= high)
                parts[j] = jnp.where(ok, parts[j], NEG)
        m = m_s[rs, :]
        top = jnp.max(functools.reduce(jnp.maximum, parts), axis=1, keepdims=True)
        new = jnp.maximum(m, jnp.broadcast_to(top, m.shape))
        parts = [jnp.exp2((x - new) * factor) for x in parts]
        scale = jnp.exp2((m - new) * factor)
        weight = jnp.concatenate([x.astype(jnp.bfloat16) for x in parts], axis=1)
        m_s[rs, :] = new
        l_s[rs, :] = l_s[rs, :] * scale + functools.reduce(jnp.add, parts)
        a_s[rs, :] = a_s[rs, :] * scale + jnp.dot(
            weight, kv[b, k0 : k0 + keys, 128:256], preferred_element_type=jnp.float32
        )

    if first_stage:
        step = 128
        for t in range(0, rows, step):
            update(0, base, t * group, step * group, 0, t + step, True, True)
    for i in range(ntiles):
        low, high = lows[i], highs[i]

        def block(b, _):
            index = lax.bitwise_xor(me - 4 * ((origin + b) >> 2), (origin + b) & 3)
            first = index * rows

            @pl.when((index >= 0) & (index < me) & (first + rows > low))
            def _():
                @pl.when(high <= first)
                def _():
                    for r in range(0, tile * group, sub):
                        update(b, first, i * tile * group + r, sub, 0, rows, False, False)

                @pl.when(high > first)
                def _():
                    for r in range(0, tile * group, sub):
                        update(b, first, i * tile * group + r, sub, 0, rows, True, False)

            return 0

        lax.fori_loop(1 if first_stage else 0, count, block, 0)
    if last_stage:
        total = jnp.sum(l_s[...], axis=1, keepdims=True)
        refs[0][...] = (a_s[...] / total).astype(refs[0].dtype)


def stage(me, doc_lengths, q, blocks, origin, state, last, rows, group, tile=256, sub=2048):
    n, hdim = q.shape
    factor = 1.4426950408889634 / hdim**0.5
    vmem = pl.BlockSpec(memory_space=pltpu.VMEM)
    smem = pl.BlockSpec(memory_space=pltpu.SMEM)
    held = [pltpu.VMEM((n, hdim), jnp.float32)] * 3
    scratch = [pltpu.VMEM((len(blocks), rows, 2 * hdim), jnp.bfloat16), pltpu.VMEM((rows, hdim), jnp.int32)]
    outs = [pltpu.VMEM((n, hdim), jnp.bfloat16)] if last else []
    nin = 3 + len(blocks)
    result = pl.pallas_call(
        functools.partial(kernel, state is None, last, origin, rows, group, tile, sub, factor),
        out_shape=outs + held,
        in_specs=[smem, smem, vmem] + [pl.BlockSpec(memory_space=pl.ANY)] * len(blocks) + [vmem] * (0 if state is None else 3),
        out_specs=[vmem] * (len(outs) + 3),
        input_output_aliases={} if state is None else {nin + i: len(outs) + i for i in range(3)},
        scratch_shapes=scratch + [pltpu.SemaphoreType.DMA((len(blocks),))],
        compiler_params=pltpu.CompilerParams(vmem_limit_bytes=28 << 20),
        cost_estimate=pl.CostEstimate(
            flops=2_000_000_000 * len(blocks), bytes_accessed=300_000 * len(blocks), transcendentals=2_000_000 * len(blocks)
        ),
    )(me, doc_lengths, q, *blocks, *(state or ()))
    return result[0] if last else tuple(result)


def on_device(queries, keys, values, doc_lengths):
    rows, group, hdim = queries.shape
    count = lax.axis_size("ctx")
    heads = lax.axis_size("head")
    me = lax.axis_index("ctx").reshape(1)
    own = jnp.concatenate([keys[:, 0, :], values[:, 0, :]], axis=1)

    def swap(x, bit):
        return lax.ppermute(x, "ctx", [(i, i ^ bit) for i in range(count)])

    def plane(x):
        return lax.ppermute(x, "ctx", [(i, i + 4) for i in range(count - 4)])

    q = pltpu.with_memory_space_constraint(queries.reshape(rows * group, hdim), pltpu.VMEM)
    z1 = plane(own)
    x0 = swap(own, 2)
    c0 = swap(own, 1)
    state = stage(me, doc_lengths, q, [own, c0], 0, None, False, rows, group)
    z1, x0, state = lax.optimization_barrier((z1, x0, state))
    z2 = plane(z1)
    x1 = swap(z1, 2)
    xc0 = swap(x0, 1)
    c1 = swap(z1, 1)
    state = stage(me, doc_lengths, q, [x0, xc0, z1, c1], 2, state, False, rows, group)
    z2, x1, state = lax.optimization_barrier((z2, x1, state))
    x2 = lax.ppermute(z2, "ctx", [(i, i ^ 2) for i in range(count) if i & 2])
    xc1 = swap(x1, 1)
    c2 = swap(z2, 1)
    state = stage(me, doc_lengths, q, [x1, xc1, z2, c2], 6, state, False, rows, group)
    x2, state = lax.optimization_barrier((x2, state))
    xc2 = swap(x2, 1)
    out = stage(me, doc_lengths, q, [x2, xc2], 10, state, True, rows, group)
    out = lax.all_to_all(out.reshape(heads, -1, hdim), "head", split_axis=0, concat_axis=0, tiled=True)
    out = out.reshape(heads, rows // heads, group, hdim)
    return jnp.transpose(out, (1, 0, 2, 3)).reshape(rows // heads, heads * group * hdim)


def solution(mesh):
    placed = (P("ctx", "head", None), P("ctx", "head", None), P("ctx", "head", None), P())
    return jax.shard_map(
        on_device, mesh=mesh, in_specs=placed, out_specs=P(("ctx", "head"), None), check_vma=False
    )
```

```python
import functools

import jax
import jax.numpy as jnp
from jax import lax
from jax.experimental import pallas as pl
from jax.experimental.pallas import tpu as pltpu
from jax.sharding import PartitionSpec as P

NEG = -1e30
NT = (((1,), (1,)), ((), ()))
HALF = 256
GROUP = 256
VMEM = pl.BlockSpec(memory_space=pltpu.VMEM)
SMEM = pl.BlockSpec(memory_space=pltpu.SMEM)


def first_doc(base, len_ref, visit):
    def doc(d, carry):
        end, low, high = carry
        length = len_ref[d]
        visit(end, length)
        here = (end <= base) & (end + length > base)
        return end + length, jnp.where(here, end, low), jnp.where(here, end + length, high)

    _, low, high = lax.fori_loop(0, len_ref.shape[0], doc, (jnp.int32(0),) * 3)
    return low, high


def own_kernel(rows, group, factor, me_ref, len_ref, q_hbm, kv_ref, qx_ref, m_ref, la_ref, q_s, start_s, sem):
    n, hdim = q_s.shape
    copy = pltpu.make_async_copy(q_hbm, q_s, sem)
    copy.start()
    base = me_ref[0] * rows
    tokens = base + lax.broadcasted_iota(jnp.int32, (rows, hdim), 0)
    start_s[...] = jnp.zeros_like(start_s)

    def visit(start, length):
        @pl.when((start < base + rows) & (start + length > base))
        def _():
            start_s[...] = jnp.where(tokens >= start, start, start_s[...])

    _, high = first_doc(base, len_ref, visit)
    lane = lax.broadcasted_iota(jnp.int32, (1, hdim), 1)
    token = base + lax.broadcasted_iota(jnp.int32, (n, hdim), 0) // group
    flag = (lane == 0) | ((lane == 1) & (token >= high))
    qx_ref[:, hdim : 2 * hdim] = jnp.where(flag, 1.0, 0.0).astype(jnp.bfloat16)
    copy.wait()
    qx_ref[:, 0:hdim] = q_s[...]
    step = 128
    for t in range(0, rows, step):
        keys, many = t + step, step * group
        rs = pl.ds(t * group, many)
        s = lax.dot_general(q_s[rs, :], kv_ref[0:keys, 0:hdim], NT, preferred_element_type=jnp.float32)
        spread = lambda x: jnp.broadcast_to(x[:, None, :], (step, group, hdim)).reshape(many, hdim)
        low = spread(start_s[pl.ds(t, step), :])
        now = spread(base + t + lax.broadcasted_iota(jnp.int32, (step, hdim), 0))
        parts = []
        for j in range(0, keys, hdim):
            pos = base + j + lane
            ok = pos >= low
            if j + hdim > t:
                ok = ok & (pos <= now)
            parts.append(jnp.where(ok, s[:, j : j + hdim], NEG))
        top = jnp.max(functools.reduce(jnp.maximum, parts), axis=1, keepdims=True)
        top = jnp.broadcast_to(top, (many, hdim))
        parts = [jnp.exp2((x - top) * factor) for x in parts]
        total = jnp.sum(functools.reduce(jnp.add, parts), axis=1, keepdims=True)
        weight = jnp.concatenate([x.astype(jnp.bfloat16) for x in parts], axis=1)
        m_ref[rs, :] = top
        la_ref[rs, 0:hdim] = jnp.broadcast_to(total, (many, hdim))
        la_ref[rs, hdim : 2 * hdim] = jnp.dot(
            weight, kv_ref[0:keys, hdim : 2 * hdim], preferred_element_type=jnp.float32
        )


def later_kernel(origin, count, last, rows, factor, me_ref, len_ref, qx_ref, *refs):
    blocks, refs = refs[:count], refs[count + 2 :]
    out_ref = refs[0] if last else None
    m_ref, la_ref, kx, vx = refs[-4:]
    n = qx_ref.shape[0]
    hdim = qx_ref.shape[1] // 2
    me = me_ref[0]
    low, _ = first_doc(me * rows, len_ref, lambda start, length: None)
    groups = n // GROUP
    steps = groups * (rows // HALF)

    def index_of(code):
        return lax.bitwise_xor(me - 4 * (code >> 2), code & 3)

    def needed(index):
        return (index >= 0) & (index < me) & (index * rows + rows > low)

    lane = lax.broadcasted_iota(jnp.int32, (rows, hdim), 1)
    place = lax.broadcasted_iota(jnp.int32, (rows, hdim), 0)
    for b in range(count):
        index = index_of(jnp.int32(origin + b))

        @pl.when(needed(index))
        def _():
            early = jnp.where(place + index * rows >= low, 0.0, NEG)
            kx[b, :, 0:hdim] = blocks[b][:, 0:hdim]
            kx[b, :, hdim : 2 * hdim] = jnp.where(lane == 0, early, jnp.where(lane == 1, NEG, 0.0)).astype(jnp.bfloat16)
            vx[b, :, 0:hdim] = jnp.ones((rows, hdim), jnp.bfloat16)
            vx[b, :, hdim : 2 * hdim] = blocks[b][:, hdim : 2 * hdim]

    def attend(b, score, mixed):
        def soften(s, g):
            rs = pl.ds(g * GROUP, GROUP)
            m = m_ref[rs, :]
            s0, s1 = s[:, 0:hdim], s[:, hdim : 2 * hdim]
            top = jnp.max(jnp.maximum(s0, s1), axis=1, keepdims=True)
            new = jnp.maximum(m, jnp.broadcast_to(top, m.shape))
            weight = jnp.concatenate([jnp.exp2((x - new) * factor).astype(jnp.bfloat16) for x in (s0, s1)], axis=1)
            m_ref[rs, :] = new
            return weight, jnp.exp2((m - new) * factor)

        def flush(o, g, scale):
            rs = pl.ds(g * GROUP, GROUP)
            for j in (0, hdim):
                la_ref[rs, j : j + hdim] = la_ref[rs, j : j + hdim] * scale + o[:, j : j + hdim]

        def multiply(acc, lhs, step):
            fresh = step // groups if step % groups == 0 else None
            pltpu.matmul_acc_lhs(acc, lhs, load_staged_rhs=fresh)

        for h in range(rows // HALF):
            pltpu.matmul_push_rhs(kx[b, h * HALF : (h + 1) * HALF, :], h, 0, transpose=True)
            pltpu.matmul_push_rhs(vx[b, h * HALF : (h + 1) * HALF, :], h, 1)
        done = []
        for t in range(-1, steps + 2):
            if t + 1 < steps:
                multiply(score[(t + 1) % 2], qx_ref[pl.ds((t + 1) % groups * GROUP, GROUP), :], t + 1)
            if 0 <= t < steps:
                done.append(soften(pltpu.matmul_pop(score[t % 2]), t % groups))
            if 1 <= t < steps + 1:
                multiply(mixed[(t - 1) % 2], done[t - 1][0], t - 1)
            if 2 <= t:
                flush(pltpu.matmul_pop(mixed[(t - 2) % 2]), (t - 2) % groups, done[t - 2][1])

    def run(s0, s1, p0, p1):
        @pl.loop(0, count)
        def _(b):
            @pl.when(needed(index_of(origin + b)))
            def _():
                attend(b, (s0, s1), (p0, p1))

    score = pltpu.ACC(mxu_id=0)((GROUP, 2 * hdim), jnp.float32)
    mixed = pltpu.ACC(mxu_id=1)((GROUP, 2 * hdim), jnp.float32)
    pl.run_scoped(run, score, score, mixed, mixed)
    if last:
        out_ref[...] = (la_ref[:, hdim : 2 * hdim] / la_ref[:, 0:hdim]).astype(out_ref.dtype)


def own_stage(me, doc_lengths, q, kv, rows, group, factor):
    n, hdim = q.shape
    return pl.pallas_call(
        functools.partial(own_kernel, rows, group, factor),
        out_shape=[
            pltpu.VMEM((n, 2 * hdim), jnp.bfloat16),
            pltpu.VMEM((n, hdim), jnp.float32),
            pltpu.VMEM((n, 2 * hdim), jnp.float32),
        ],
        in_specs=[SMEM, SMEM, pl.BlockSpec(memory_space=pl.ANY), VMEM],
        out_specs=[VMEM] * 3,
        scratch_shapes=[
            pltpu.VMEM((n, hdim), jnp.bfloat16),
            pltpu.VMEM((rows, hdim), jnp.int32),
            pltpu.SemaphoreType.DMA(()),
        ],
        compiler_params=pltpu.CompilerParams(vmem_limit_bytes=28 << 20),
        cost_estimate=pl.CostEstimate(flops=1_500_000_000, bytes_accessed=1_500_000, transcendentals=1_500_000),
    )(me, doc_lengths, q, kv)


def later_stage(me, doc_lengths, state, blocks, origin, last, rows, factor):
    qx, m, la = state
    n, hdim = m.shape
    count = len(blocks)
    held = [pltpu.VMEM((n, hdim), jnp.float32), pltpu.VMEM((n, 2 * hdim), jnp.float32)]
    outs = [pltpu.VMEM((n, hdim), jnp.bfloat16)] if last else []
    result = pl.pallas_call(
        functools.partial(later_kernel, origin, count, last, rows, factor),
        out_shape=outs + held,
        in_specs=[SMEM, SMEM] + [VMEM] * (count + 3),
        out_specs=[VMEM] * (len(outs) + 2),
        input_output_aliases={3 + count + i: len(outs) + i for i in range(2)},
        scratch_shapes=[pltpu.VMEM((count, rows, 2 * hdim), jnp.bfloat16)] * 2,
        compiler_params=pltpu.CompilerParams(vmem_limit_bytes=28 << 20),
        cost_estimate=pl.CostEstimate(
            flops=2_000_000_000 * count, bytes_accessed=300_000 * count, transcendentals=2_000_000 * count
        ),
    )(me, doc_lengths, qx, *blocks, m, la)
    return result[0] if last else (qx, *result)


def on_device(queries, keys, values, doc_lengths):
    rows, group, hdim = queries.shape
    count = lax.axis_size("ctx")
    heads = lax.axis_size("head")
    factor = 1.4426950408889634 / hdim**0.5
    me = lax.axis_index("ctx").reshape(1)
    own = jnp.concatenate([keys[:, 0, :], values[:, 0, :]], axis=1)

    def swap(x, bit):
        return lax.ppermute(x, "ctx", [(i, i ^ bit) for i in range(count)])

    def plane(x):
        return lax.ppermute(x, "ctx", [(i, i + 4) for i in range(count - 4)])

    z1 = plane(own)
    x0 = swap(own, 2)
    c0 = swap(own, 1)
    state = own_stage(me, doc_lengths, queries.reshape(rows * group, hdim), own, rows, group, factor)
    z1, x0, c0, state = lax.optimization_barrier((z1, x0, c0, state))
    z2 = plane(z1)
    x1 = swap(z1, 2)
    xc0 = swap(x0, 1)
    c1 = swap(z1, 1)
    state = later_stage(me, doc_lengths, state, [c0, x0, xc0, z1, c1], 1, False, rows, factor)
    z2, x1, state = lax.optimization_barrier((z2, x1, state))
    x2 = lax.ppermute(z2, "ctx", [(i, i ^ 2) for i in range(count) if i & 2])
    xc1 = swap(x1, 1)
    c2 = swap(z2, 1)
    state = later_stage(me, doc_lengths, state, [x1, xc1, z2, c2], 6, False, rows, factor)
    x2, state = lax.optimization_barrier((x2, state))
    xc2 = swap(x2, 1)
    out = later_stage(me, doc_lengths, state, [x2, xc2], 10, True, rows, factor)
    out = lax.all_to_all(out.reshape(heads, -1, hdim), "head", split_axis=0, concat_axis=0, tiled=True)
    out = out.reshape(heads, rows // heads, group, hdim)
    return jnp.transpose(out, (1, 0, 2, 3)).reshape(rows // heads, heads * group * hdim)


def solution(mesh):
    placed = (P("ctx", "head", None), P("ctx", "head", None), P("ctx", "head", None), P())

    return jax.shard_map(
        on_device, mesh=mesh, in_specs=placed, out_specs=P(("ctx", "head"), None), check_vma=False
    )
```

```python
import functools

import jax
import jax.numpy as jnp
from jax import lax
from jax.experimental import pallas as pl
from jax.experimental.pallas import tpu as pltpu
from jax.sharding import PartitionSpec as P

NEG = -1e30
NT = (((1,), (1,)), ((), ()))
HALF = 256
GROUP = 256
EARLY = 2
VMEM = pl.BlockSpec(memory_space=pltpu.VMEM)
SMEM = pl.BlockSpec(memory_space=pltpu.SMEM)


def first_doc(base, len_ref, visit):
    def doc(d, carry):
        end, low, high = carry
        length = len_ref[d]
        visit(end, length)
        here = (end <= base) & (end + length > base)
        return end + length, jnp.where(here, end, low), jnp.where(here, end + length, high)

    _, low, high = lax.fori_loop(0, len_ref.shape[0], doc, (jnp.int32(0),) * 3)
    return low, high


def own_kernel(rows, group, factor, me_ref, len_ref, q_hbm, kv_ref, qx_ref, m_ref, la_ref, q_s, start_s, sem):
    n, hdim = q_s.shape
    copy = pltpu.make_async_copy(q_hbm, q_s, sem)
    copy.start()
    base = me_ref[0] * rows
    tokens = base + lax.broadcasted_iota(jnp.int32, (rows, hdim), 0)
    start_s[...] = jnp.zeros_like(start_s)

    def visit(start, length):
        @pl.when((start < base + rows) & (start + length > base))
        def _():
            start_s[...] = jnp.where(tokens >= start, start, start_s[...])

    _, high = first_doc(base, len_ref, visit)
    lane = lax.broadcasted_iota(jnp.int32, (1, hdim), 1)
    token = base + lax.broadcasted_iota(jnp.int32, (n, hdim), 0) // group
    flag = (lane == 0) | ((lane == 1) & (token >= high))
    qx_ref[:, hdim : 2 * hdim] = jnp.where(flag, 1.0, 0.0).astype(jnp.bfloat16)
    copy.wait()
    qx_ref[:, 0:hdim] = q_s[...]
    step = 128
    for t in range(0, rows, step):
        keys, many = t + step, step * group
        rs = pl.ds(t * group, many)
        s = lax.dot_general(q_s[rs, :], kv_ref[0:keys, 0:hdim], NT, preferred_element_type=jnp.float32)
        spread = lambda x: jnp.broadcast_to(x[:, None, :], (step, group, hdim)).reshape(many, hdim)
        low = spread(start_s[pl.ds(t, step), :])
        now = spread(base + t + lax.broadcasted_iota(jnp.int32, (step, hdim), 0))
        parts = []
        for j in range(0, keys, hdim):
            pos = base + j + lane
            ok = pos >= low
            if j + hdim > t:
                ok = ok & (pos <= now)
            parts.append(jnp.where(ok, s[:, j : j + hdim], NEG))
        top = jnp.max(functools.reduce(jnp.maximum, parts), axis=1, keepdims=True)
        top = jnp.broadcast_to(top, (many, hdim))
        parts = [jnp.exp2((x - top) * factor) for x in parts]
        total = jnp.sum(functools.reduce(jnp.add, parts), axis=1, keepdims=True)
        weight = jnp.concatenate([x.astype(jnp.bfloat16) for x in parts], axis=1)
        m_ref[rs, :] = top
        la_ref[rs, 0:hdim] = jnp.broadcast_to(total, (many, hdim))
        la_ref[rs, hdim : 2 * hdim] = jnp.dot(
            weight, kv_ref[0:keys, hdim : 2 * hdim], preferred_element_type=jnp.float32
        )


def later_kernel(origin, count, skip, limit, last, rows, factor, me_ref, len_ref, qx_ref, *refs):
    blocks, refs = refs[:count], refs[count + 2 :]
    out_ref = refs[0] if last else None
    m_ref, la_ref, kx, vx = refs[-4:]
    n = qx_ref.shape[0]
    hdim = qx_ref.shape[1] // 2
    me = me_ref[0]
    low, _ = first_doc(me * rows, len_ref, lambda start, length: None)
    groups = n // GROUP
    steps = groups * (rows // HALF)

    def index_of(code):
        return lax.bitwise_xor(me - 4 * (code >> 2), code & 3)

    def needed(index):
        return (index >= 0) & (index < me) & (index * rows + rows > low)

    lane = lax.broadcasted_iota(jnp.int32, (rows, hdim), 1)
    place = lax.broadcasted_iota(jnp.int32, (rows, hdim), 0)
    for b in range(count):
        index = index_of(jnp.int32(origin + b))

        @pl.when(needed(index))
        def _():
            early = jnp.where(place + index * rows >= low, 0.0, NEG)
            kx[b, :, 0:hdim] = blocks[b][:, 0:hdim]
            kx[b, :, hdim : 2 * hdim] = jnp.where(lane == 0, early, jnp.where(lane == 1, NEG, 0.0)).astype(jnp.bfloat16)
            vx[b, :, 0:hdim] = jnp.ones((rows, hdim), jnp.bfloat16)
            vx[b, :, hdim : 2 * hdim] = blocks[b][:, hdim : 2 * hdim]

    def attend(b, score, mixed):
        def soften(s, g):
            rs = pl.ds(g * GROUP, GROUP)
            m = m_ref[rs, :]
            s0, s1 = s[:, 0:hdim], s[:, hdim : 2 * hdim]
            top = jnp.max(jnp.maximum(s0, s1), axis=1, keepdims=True)
            new = jnp.maximum(m, jnp.broadcast_to(top, m.shape))
            weight = jnp.concatenate([jnp.exp2((x - new) * factor).astype(jnp.bfloat16) for x in (s0, s1)], axis=1)
            m_ref[rs, :] = new
            return weight, jnp.exp2((m - new) * factor)

        def flush(o, g, scale):
            rs = pl.ds(g * GROUP, GROUP)
            for j in (0, hdim):
                la_ref[rs, j : j + hdim] = la_ref[rs, j : j + hdim] * scale + o[:, j : j + hdim]

        def multiply(acc, lhs, step):
            fresh = step // groups if step % groups == 0 else None
            pltpu.matmul_acc_lhs(acc, lhs, load_staged_rhs=fresh)

        for h in range(rows // HALF):
            pltpu.matmul_push_rhs(kx[b, h * HALF : (h + 1) * HALF, :], h, 0, transpose=True)
            pltpu.matmul_push_rhs(vx[b, h * HALF : (h + 1) * HALF, :], h, 1)
        done = []
        for t in range(-1, steps + 2):
            if t + 1 < steps:
                multiply(score[(t + 1) % 2], qx_ref[pl.ds((t + 1) % groups * GROUP, GROUP), :], t + 1)
            if 0 <= t < steps:
                done.append(soften(pltpu.matmul_pop(score[t % 2]), t % groups))
            if 1 <= t < steps + 1:
                multiply(mixed[(t - 1) % 2], done[t - 1][0], t - 1)
            if 2 <= t:
                flush(pltpu.matmul_pop(mixed[(t - 2) % 2]), (t - 2) % groups, done[t - 2][1])

    def run(s0, s1, p0, p1):
        def one(b, rank):
            need = needed(index_of(origin + b))

            @pl.when(need & (rank < limit) & ((rank >= skip[0]) | (b >= skip[1])))
            def _():
                attend(b, (s0, s1), (p0, p1))

            return rank + need.astype(jnp.int32)

        lax.fori_loop(0, count, one, jnp.int32(0))

    score = pltpu.ACC(mxu_id=0)((GROUP, 2 * hdim), jnp.float32)
    mixed = pltpu.ACC(mxu_id=1)((GROUP, 2 * hdim), jnp.float32)
    pl.run_scoped(run, score, score, mixed, mixed)
    if last:
        group = n // rows
        m_ref[...] = la_ref[:, hdim : 2 * hdim] / la_ref[:, 0:hdim]
        for h in range(group):
            rs = pl.ds(h, rows, stride=group)
            out_ref[:, h * hdim : (h + 1) * hdim] = m_ref[rs, :].astype(out_ref.dtype)


def own_stage(me, doc_lengths, q, kv, rows, group, factor):
    n, hdim = q.shape
    return pl.pallas_call(
        functools.partial(own_kernel, rows, group, factor),
        out_shape=[
            pltpu.VMEM((n, 2 * hdim), jnp.bfloat16),
            pltpu.VMEM((n, hdim), jnp.float32),
            pltpu.VMEM((n, 2 * hdim), jnp.float32),
        ],
        in_specs=[SMEM, SMEM, pl.BlockSpec(memory_space=pltpu.HBM), VMEM],
        out_specs=[VMEM] * 3,
        scratch_shapes=[
            pltpu.VMEM((n, hdim), jnp.bfloat16),
            pltpu.VMEM((rows, hdim), jnp.int32),
            pltpu.SemaphoreType.DMA(()),
        ],
        compiler_params=pltpu.CompilerParams(vmem_limit_bytes=28 << 20),
        cost_estimate=pl.CostEstimate(flops=1_500_000_000, bytes_accessed=1_500_000, transcendentals=1_500_000),
    )(me, doc_lengths, q, kv)


def later_stage(me, doc_lengths, state, blocks, origin, rows, factor, skip=(0, 0), limit=99, last=False):
    qx, m, la = state
    n, hdim = m.shape
    count = len(blocks)
    held = [pltpu.VMEM((n, hdim), jnp.float32), pltpu.VMEM((n, 2 * hdim), jnp.float32)]
    outs = [pltpu.VMEM((rows, n // rows * hdim), jnp.bfloat16)] if last else []
    result = pl.pallas_call(
        functools.partial(later_kernel, origin, count, skip, limit, last, rows, factor),
        out_shape=outs + held,
        in_specs=[SMEM, SMEM] + [VMEM] * (count + 3),
        out_specs=[VMEM] * (len(outs) + 2),
        input_output_aliases={3 + count + i: len(outs) + i for i in range(2)},
        scratch_shapes=[pltpu.VMEM((count, rows, 2 * hdim), jnp.bfloat16)] * 2,
        compiler_params=pltpu.CompilerParams(vmem_limit_bytes=28 << 20),
        cost_estimate=pl.CostEstimate(
            flops=2_000_000_000 * count, bytes_accessed=300_000 * count, transcendentals=2_000_000 * count
        ),
    )(me, doc_lengths, qx, *blocks, m, la)
    return result[0] if last else (qx, *result)


def on_device(queries, keys, values, doc_lengths):
    rows, group, hdim = queries.shape
    count = lax.axis_size("ctx")
    factor = 1.4426950408889634 / hdim**0.5
    me = lax.axis_index("ctx").reshape(1)
    own = jnp.concatenate([keys[:, 0, :], values[:, 0, :]], axis=1)

    def swap(x, bit):
        return lax.ppermute(x, "ctx", [(i, i ^ bit) for i in range(count)])

    def plane(x):
        return lax.ppermute(x, "ctx", [(i, i + 4) for i in range(count - 4)])

    z1 = plane(own)
    x0 = swap(own, 2)
    c0 = swap(own, 1)
    q = pltpu.with_memory_space_constraint(queries.reshape(rows * group, hdim), pltpu.HBM)
    state = own_stage(me, doc_lengths, q, own, rows, group, factor)
    z1, x0, c0, state = lax.optimization_barrier((z1, x0, c0, state))
    z2 = plane(z1)
    x1 = swap(z1, 2)
    xc0 = swap(x0, 1)
    c1 = swap(z1, 1)
    near = [c0, x0, xc0, z1, c1]
    state = later_stage(me, doc_lengths, state, near, 1, rows, factor, limit=EARLY)
    z2, x1, state = lax.optimization_barrier((z2, x1, state))
    x2 = lax.ppermute(z2, "ctx", [(i, i ^ 2) for i in range(count) if i & 2])
    xc1 = swap(x1, 1)
    c2 = swap(z2, 1)
    state = later_stage(me, doc_lengths, state, near + [x1, xc1, z2, c2], 1, rows, factor, skip=(EARLY, len(near)))
    x2, state = lax.optimization_barrier((x2, state))
    xc2 = swap(x2, 1)
    out = later_stage(me, doc_lengths, state, [x2, xc2], 10, rows, factor, last=True)
    return lax.all_to_all(out, "head", split_axis=0, concat_axis=1, tiled=True)


def solution(mesh):
    placed = (P("ctx", "head", None), P("ctx", "head", None), P("ctx", "head", None), P())

    return jax.shard_map(
        on_device, mesh=mesh, in_specs=placed, out_specs=P(("ctx", "head"), None), check_vma=False
    )
```

```python
import functools

import jax
import jax.numpy as jnp
from jax import lax
from jax.experimental import pallas as pl
from jax.experimental.pallas import tpu as pltpu
from jax.sharding import PartitionSpec as P

NEG = -1e30
NT = (((1,), (1,)), ((), ()))
HALF = 256
GROUP = 256
EARLY = 2
VMEM = pl.BlockSpec(memory_space=pltpu.VMEM)
SMEM = pl.BlockSpec(memory_space=pltpu.SMEM)


def first_doc(base, len_ref, visit):
    def doc(d, carry):
        end, low, high = carry
        length = len_ref[d]
        if visit is not None:
            visit(end, length)
        here = (end <= base) & (end + length > base)
        return end + length, jnp.where(here, end, low), jnp.where(here, end + length, high)

    _, low, high = lax.fori_loop(0, len_ref.shape[0], doc, (jnp.int32(0),) * 3, unroll=visit is None)
    return low, high


def own_kernel(rows, group, factor, me_ref, len_ref, q_hbm, kv_ref, qx_ref, m_ref, la_ref, q_s, start_s, sem):
    n, hdim = q_s.shape
    copy = pltpu.make_async_copy(q_hbm, q_s, sem)
    copy.start()
    base = me_ref[0] * rows
    tokens = base + lax.broadcasted_iota(jnp.int32, (rows, hdim), 0)
    start_s[...] = jnp.zeros_like(start_s)

    def visit(start, length):
        @pl.when((start < base + rows) & (start + length > base))
        def _():
            start_s[...] = jnp.where(tokens >= start, start, start_s[...])

    _, high = first_doc(base, len_ref, visit)
    lane = lax.broadcasted_iota(jnp.int32, (1, hdim), 1)
    token = base + lax.broadcasted_iota(jnp.int32, (n, hdim), 0) // group
    flag = (lane == 0) | ((lane == 1) & (token >= high))
    qx_ref[:, hdim : 2 * hdim] = jnp.where(flag, 1.0, 0.0).astype(jnp.bfloat16)
    copy.wait()
    qx_ref[:, 0:hdim] = q_s[...]
    step = 128
    for t in range(0, rows, step):
        keys, many = t + step, step * group
        rs = pl.ds(t * group, many)
        s = lax.dot_general(q_s[rs, :], kv_ref[0:keys, 0:hdim], NT, preferred_element_type=jnp.float32)
        spread = lambda x: jnp.broadcast_to(x[:, None, :], (step, group, hdim)).reshape(many, hdim)
        low = spread(start_s[pl.ds(t, step), :])
        now = spread(base + t + lax.broadcasted_iota(jnp.int32, (step, hdim), 0))
        parts = []
        for j in range(0, keys, hdim):
            pos = base + j + lane
            ok = pos >= low
            if j + hdim > t:
                ok = ok & (pos <= now)
            parts.append(jnp.where(ok, s[:, j : j + hdim], NEG))
        top = jnp.max(functools.reduce(jnp.maximum, parts), axis=1, keepdims=True)
        top = jnp.broadcast_to(top, (many, hdim))
        parts = [jnp.exp2((x - top) * factor) for x in parts]
        total = jnp.sum(functools.reduce(jnp.add, parts), axis=1, keepdims=True)
        weight = jnp.concatenate([x.astype(jnp.bfloat16) for x in parts], axis=1)
        m_ref[rs, :] = top
        la_ref[rs, 0:hdim] = jnp.broadcast_to(total, (many, hdim))
        la_ref[rs, hdim : 2 * hdim] = jnp.dot(
            weight, kv_ref[0:keys, hdim : 2 * hdim], preferred_element_type=jnp.float32
        )


def later_kernel(origin, count, skip, limit, last, rows, factor, me_ref, len_ref, qx_ref, *refs):
    blocks, refs = refs[:count], refs[count + 2 :]
    out_ref = refs[0] if last else None
    m_ref, la_ref, kx, vx = refs[-4:]
    n = qx_ref.shape[0]
    hdim = qx_ref.shape[1] // 2
    me = me_ref[0]
    low, _ = first_doc(me * rows, len_ref, None)
    groups = n // GROUP
    steps = groups * (rows // HALF)

    def index_of(code):
        return lax.bitwise_xor(me - 4 * (code >> 2), code & 3)

    def needed(index):
        return (index >= 0) & (index < me) & (index * rows + rows > low)

    lane = lax.broadcasted_iota(jnp.int32, (rows, hdim), 1)
    place = lax.broadcasted_iota(jnp.int32, (rows, hdim), 0)
    for b in range(count):
        index = index_of(jnp.int32(origin + b))

        @pl.when(needed(index))
        def _():
            early = jnp.where(place + index * rows >= low, 0.0, NEG)
            kx[b, :, 0:hdim] = blocks[b][:, 0:hdim]
            kx[b, :, hdim : 2 * hdim] = jnp.where(lane == 0, early, jnp.where(lane == 1, NEG, 0.0)).astype(jnp.bfloat16)
            vx[b, :, 0:hdim] = jnp.ones((rows, hdim), jnp.bfloat16)
            vx[b, :, hdim : 2 * hdim] = blocks[b][:, hdim : 2 * hdim]

    def attend(b, score, mixed):
        def soften(s, g):
            rs = pl.ds(g * GROUP, GROUP)
            m = m_ref[rs, :]
            s0, s1 = s[:, 0:hdim], s[:, hdim : 2 * hdim]
            top = jnp.max(jnp.maximum(s0, s1), axis=1, keepdims=True)
            new = jnp.maximum(m, jnp.broadcast_to(top, m.shape))
            weight = jnp.concatenate([jnp.exp2((x - new) * factor).astype(jnp.bfloat16) for x in (s0, s1)], axis=1)
            m_ref[rs, :] = new
            return weight, jnp.exp2((m - new) * factor)

        def flush(o, g, scale):
            rs = pl.ds(g * GROUP, GROUP)
            for j in (0, hdim):
                la_ref[rs, j : j + hdim] = la_ref[rs, j : j + hdim] * scale + o[:, j : j + hdim]

        def multiply(acc, lhs, step):
            fresh = step // groups if step % groups == 0 else None
            pltpu.matmul_acc_lhs(acc, lhs, load_staged_rhs=fresh)

        for h in range(rows // HALF):
            pltpu.matmul_push_rhs(kx[b, h * HALF : (h + 1) * HALF, :], h, 0, transpose=True)
            pltpu.matmul_push_rhs(vx[b, h * HALF : (h + 1) * HALF, :], h, 1)
        done = []
        for t in range(-1, steps + 2):
            if t + 1 < steps:
                multiply(score[(t + 1) % 2], qx_ref[pl.ds((t + 1) % groups * GROUP, GROUP), :], t + 1)
            if 0 <= t < steps:
                done.append(soften(pltpu.matmul_pop(score[t % 2]), t % groups))
            if 1 <= t < steps + 1:
                multiply(mixed[(t - 1) % 2], done[t - 1][0], t - 1)
            if 2 <= t:
                flush(pltpu.matmul_pop(mixed[(t - 2) % 2]), (t - 2) % groups, done[t - 2][1])

    def run(s0, s1, p0, p1):
        def one(b, rank):
            need = needed(index_of(origin + b))

            @pl.when(need & (rank < limit) & ((rank >= skip[0]) | (b >= skip[1])))
            def _():
                attend(b, (s0, s1), (p0, p1))

            return rank + need.astype(jnp.int32)

        lax.fori_loop(0, count, one, jnp.int32(0))

    score = pltpu.ACC(mxu_id=0)((GROUP, 2 * hdim), jnp.float32)
    mixed = pltpu.ACC(mxu_id=1)((GROUP, 2 * hdim), jnp.float32)
    pl.run_scoped(run, score, score, mixed, mixed)
    if last:
        group = n // rows
        m_ref[...] = la_ref[:, hdim : 2 * hdim] / la_ref[:, 0:hdim]
        for h in range(group):
            rs = pl.ds(h, rows, stride=group)
            out_ref[:, h * hdim : (h + 1) * hdim] = m_ref[rs, :].astype(out_ref.dtype)


def own_stage(me, doc_lengths, q, kv, rows, group, factor):
    n, hdim = q.shape
    return pl.pallas_call(
        functools.partial(own_kernel, rows, group, factor),
        out_shape=[
            pltpu.VMEM((n, 2 * hdim), jnp.bfloat16),
            pltpu.VMEM((n, hdim), jnp.float32),
            pltpu.VMEM((n, 2 * hdim), jnp.float32),
        ],
        in_specs=[SMEM, SMEM, pl.BlockSpec(memory_space=pltpu.HBM), VMEM],
        out_specs=[VMEM] * 3,
        scratch_shapes=[
            pltpu.VMEM((n, hdim), jnp.bfloat16),
            pltpu.VMEM((rows, hdim), jnp.int32),
            pltpu.SemaphoreType.DMA(()),
        ],
        compiler_params=pltpu.CompilerParams(vmem_limit_bytes=28 << 20),
        cost_estimate=pl.CostEstimate(flops=1_500_000_000, bytes_accessed=1_500_000, transcendentals=1_500_000),
    )(me, doc_lengths, q, kv)


def later_stage(me, doc_lengths, state, blocks, origin, rows, factor, skip=(0, 0), limit=99, last=False):
    qx, m, la = state
    n, hdim = m.shape
    count = len(blocks)
    held = [pltpu.VMEM((n, hdim), jnp.float32), pltpu.VMEM((n, 2 * hdim), jnp.float32)]
    outs = [pltpu.VMEM((rows, n // rows * hdim), jnp.bfloat16)] if last else []
    result = pl.pallas_call(
        functools.partial(later_kernel, origin, count, skip, limit, last, rows, factor),
        out_shape=outs + held,
        in_specs=[SMEM, SMEM] + [VMEM] * (count + 3),
        out_specs=[VMEM] * (len(outs) + 2),
        input_output_aliases={3 + count + i: len(outs) + i for i in range(2)},
        scratch_shapes=[pltpu.VMEM((count, rows, 2 * hdim), jnp.bfloat16)] * 2,
        compiler_params=pltpu.CompilerParams(vmem_limit_bytes=28 << 20),
        cost_estimate=pl.CostEstimate(
            flops=2_000_000_000 * count, bytes_accessed=300_000 * count, transcendentals=2_000_000 * count
        ),
    )(me, doc_lengths, qx, *blocks, m, la)
    return result[0] if last else (qx, *result)


def on_device(queries, keys, values, doc_lengths):
    rows, group, hdim = queries.shape
    count = lax.axis_size("ctx")
    factor = 1.4426950408889634 / hdim**0.5
    me = lax.axis_index("ctx").reshape(1)
    own = jnp.concatenate([keys[:, 0, :], values[:, 0, :]], axis=1)

    def swap(x, bit):
        return lax.ppermute(x, "ctx", [(i, i ^ bit) for i in range(count)])

    def plane(x):
        return lax.ppermute(x, "ctx", [(i, i + 4) for i in range(count - 4)])

    z1 = plane(own)
    x0 = swap(own, 2)
    c0 = swap(own, 1)
    q = pltpu.with_memory_space_constraint(queries.reshape(rows * group, hdim), pltpu.HBM)
    state = own_stage(me, doc_lengths, q, own, rows, group, factor)
    z1, x0, c0, state = lax.optimization_barrier((z1, x0, c0, state))
    z2 = plane(z1)
    x1 = swap(z1, 2)
    xc0 = swap(x0, 1)
    c1 = swap(z1, 1)
    near = [c0, x0, xc0, z1, c1]
    state = later_stage(me, doc_lengths, state, near, 1, rows, factor, limit=EARLY)
    z2, x1, state = lax.optimization_barrier((z2, x1, state))
    x2 = lax.ppermute(z2, "ctx", [(i, i ^ 2) for i in range(count) if i & 2])
    xc2 = lax.ppermute(z2, "ctx", [(i, i ^ 3) for i in range(count) if i & 2])
    xc1 = swap(x1, 1)
    c2 = swap(z2, 1)
    state = later_stage(me, doc_lengths, state, near + [x1, xc1, z2, c2], 1, rows, factor, skip=(EARLY, len(near)))
    x2, xc2, state = lax.optimization_barrier((x2, xc2, state))
    out = later_stage(me, doc_lengths, state, [x2, xc2], 10, rows, factor, last=True)
    return lax.all_to_all(out, "head", split_axis=0, concat_axis=1, tiled=True)


def solution(mesh):
    placed = (P("ctx", "head", None), P("ctx", "head", None), P("ctx", "head", None), P())

    return jax.shard_map(
        on_device, mesh=mesh, in_specs=placed, out_specs=P(("ctx", "head"), None), check_vma=False
    )
```

```python
import functools

import jax
import jax.numpy as jnp
from jax import lax
from jax.experimental import pallas as pl
from jax.experimental.pallas import tpu as pltpu
from jax.sharding import PartitionSpec as P

NEG = -1e30
NT = (((1,), (1,)), ((), ()))
HALF = 256
GROUP = 256
EARLY = 2
VMEM = pl.BlockSpec(memory_space=pltpu.VMEM)
SMEM = pl.BlockSpec(memory_space=pltpu.SMEM)


def first_doc(base, len_ref, visit):
    def doc(d, carry):
        end, low, high = carry
        length = len_ref[d]
        if visit is not None:
            visit(end, length)
        here = (end <= base) & (end + length > base)
        return end + length, jnp.where(here, end, low), jnp.where(here, end + length, high)

    _, low, high = lax.fori_loop(0, len_ref.shape[0], doc, (jnp.int32(0),) * 3, unroll=visit is None)
    return low, high


def own_kernel(rows, group, factor, me_ref, len_ref, q_hbm, kv_ref, qx_ref, m_ref, la_ref, q_s, start_s, sem):
    n, hdim = q_s.shape
    copy = pltpu.make_async_copy(q_hbm, q_s, sem)
    copy.start()
    base = me_ref[0] * rows
    tokens = base + lax.broadcasted_iota(jnp.int32, (rows, hdim), 0)
    start_s[...] = jnp.zeros_like(start_s)

    def visit(start, length):
        @pl.when((start < base + rows) & (start + length > base))
        def _():
            start_s[...] = jnp.where(tokens >= start, start, start_s[...])

    _, high = first_doc(base, len_ref, visit)
    lane = lax.broadcasted_iota(jnp.int32, (1, hdim), 1)
    token = base + lax.broadcasted_iota(jnp.int32, (n, hdim), 0) // group
    flag = (lane == 0) | ((lane == 1) & (token >= high))
    qx_ref[:, hdim : 2 * hdim] = jnp.where(flag, 1.0, 0.0).astype(jnp.bfloat16)
    copy.wait()
    qx_ref[:, 0:hdim] = q_s[...]
    step = 128
    for t in range(0, rows, step):
        keys, many = t + step, step * group
        rs = pl.ds(t * group, many)
        s = lax.dot_general(q_s[rs, :], kv_ref[0:keys, 0:hdim], NT, preferred_element_type=jnp.float32)
        spread = lambda x: jnp.broadcast_to(x[:, None, :], (step, group, hdim)).reshape(many, hdim)
        low = spread(start_s[pl.ds(t, step), :])
        now = spread(base + t + lax.broadcasted_iota(jnp.int32, (step, hdim), 0))
        parts = []
        for j in range(0, keys, hdim):
            pos = base + j + lane
            ok = pos >= low
            if j + hdim > t:
                ok = ok & (pos <= now)
            parts.append(jnp.where(ok, s[:, j : j + hdim], NEG))
        top = jnp.max(functools.reduce(jnp.maximum, parts), axis=1, keepdims=True)
        top = jnp.broadcast_to(top, (many, hdim))
        parts = [jnp.exp2((x - top) * factor) for x in parts]
        total = jnp.sum(functools.reduce(jnp.add, parts), axis=1, keepdims=True)
        weight = jnp.concatenate([x.astype(jnp.bfloat16) for x in parts], axis=1)
        m_ref[rs, :] = top
        la_ref[rs, 0:hdim] = jnp.broadcast_to(total, (many, hdim))
        la_ref[rs, hdim : 2 * hdim] = jnp.dot(
            weight, kv_ref[0:keys, hdim : 2 * hdim], preferred_element_type=jnp.float32
        )


def later_kernel(origin, count, skip, limit, last, rows, factor, me_ref, len_ref, qx_ref, *refs):
    blocks, refs = refs[:count], refs[count + 2 :]
    out_ref = refs[0] if last else None
    m_ref, la_ref, kx, vx = refs[-4:]
    n = qx_ref.shape[0]
    hdim = qx_ref.shape[1] // 2
    me = me_ref[0]
    low, _ = first_doc(me * rows, len_ref, None)
    groups = n // GROUP
    steps = groups * (rows // HALF)

    def index_of(code):
        return lax.bitwise_xor(me - 4 * (code >> 2), code & 3)

    def needed(index):
        return (index >= 0) & (index < me) & (index * rows + rows > low)

    lane = lax.broadcasted_iota(jnp.int32, (rows, hdim), 1)
    place = lax.broadcasted_iota(jnp.int32, (rows, hdim), 0)
    for b in range(count):
        index = index_of(jnp.int32(origin + b))

        @pl.when(needed(index))
        def _():
            early = jnp.where(place + index * rows >= low, 0.0, NEG)
            kx[b, :, 0:hdim] = blocks[b][:, 0:hdim]
            kx[b, :, hdim : 2 * hdim] = jnp.where(lane == 0, early, jnp.where(lane == 1, NEG, 0.0)).astype(jnp.bfloat16)
            vx[b, :, 0:hdim] = jnp.ones((rows, hdim), jnp.bfloat16)
            vx[b, :, hdim : 2 * hdim] = blocks[b][:, hdim : 2 * hdim]

    def attend(b, score, mixed):
        def soften(s, g):
            rs = pl.ds(g * GROUP, GROUP)
            m = m_ref[rs, :]
            s0, s1 = s[:, 0:hdim], s[:, hdim : 2 * hdim]
            top = jnp.max(jnp.maximum(s0, s1), axis=1, keepdims=True)
            new = jnp.maximum(m, jnp.broadcast_to(top, m.shape))
            weight = jnp.concatenate([jnp.exp2((x - new) * factor).astype(jnp.bfloat16) for x in (s0, s1)], axis=1)
            m_ref[rs, :] = new
            return weight, jnp.exp2((m - new) * factor)

        def flush(o, g, scale):
            rs = pl.ds(g * GROUP, GROUP)
            for j in (0, hdim):
                la_ref[rs, j : j + hdim] = la_ref[rs, j : j + hdim] * scale + o[:, j : j + hdim]

        def multiply(acc, lhs, step):
            fresh = step // groups if step % groups == 0 else None
            pltpu.matmul_acc_lhs(acc, lhs, load_staged_rhs=fresh)

        for h in range(rows // HALF):
            pltpu.matmul_push_rhs(kx[b, h * HALF : (h + 1) * HALF, :], h, 0, transpose=True)
            pltpu.matmul_push_rhs(vx[b, h * HALF : (h + 1) * HALF, :], h, 1)
        done = []
        for t in range(-1, steps + 2):
            if t + 1 < steps:
                multiply(score[(t + 1) % 2], qx_ref[pl.ds((t + 1) % groups * GROUP, GROUP), :], t + 1)
            if 0 <= t < steps:
                done.append(soften(pltpu.matmul_pop(score[t % 2]), t % groups))
            if 1 <= t < steps + 1:
                multiply(mixed[(t - 1) % 2], done[t - 1][0], t - 1)
            if 2 <= t:
                flush(pltpu.matmul_pop(mixed[(t - 2) % 2]), (t - 2) % groups, done[t - 2][1])

    def run(s0, s1, p0, p1):
        def one(b, rank):
            need = needed(index_of(origin + b))

            @pl.when(need & (rank < limit) & ((rank >= skip[0]) | (b >= skip[1])))
            def _():
                attend(b, (s0, s1), (p0, p1))

            return rank + need.astype(jnp.int32)

        lax.fori_loop(0, count, one, jnp.int32(0))

    score = pltpu.ACC(mxu_id=0)((GROUP, 2 * hdim), jnp.float32)
    mixed = pltpu.ACC(mxu_id=1)((GROUP, 2 * hdim), jnp.float32)
    pl.run_scoped(run, score, score, mixed, mixed)
    if last:
        group = n // rows
        m_ref[...] = la_ref[:, hdim : 2 * hdim] / la_ref[:, 0:hdim]
        for h in range(group):
            rs = pl.ds(h, rows, stride=group)
            out_ref[:, h * hdim : (h + 1) * hdim] = m_ref[rs, :].astype(out_ref.dtype)


def own_stage(me, doc_lengths, q, kv, rows, group, factor):
    n, hdim = q.shape
    return pl.pallas_call(
        functools.partial(own_kernel, rows, group, factor),
        out_shape=[
            pltpu.VMEM((n, 2 * hdim), jnp.bfloat16),
            pltpu.VMEM((n, hdim), jnp.float32),
            pltpu.VMEM((n, 2 * hdim), jnp.float32),
        ],
        in_specs=[SMEM, SMEM, pl.BlockSpec(memory_space=pltpu.HBM), VMEM],
        out_specs=[VMEM] * 3,
        scratch_shapes=[
            pltpu.VMEM((n, hdim), jnp.bfloat16),
            pltpu.VMEM((rows, hdim), jnp.int32),
            pltpu.SemaphoreType.DMA(()),
        ],
        compiler_params=pltpu.CompilerParams(vmem_limit_bytes=28 << 20),
        cost_estimate=pl.CostEstimate(flops=1_500_000_000, bytes_accessed=1_500_000, transcendentals=1_500_000),
    )(me, doc_lengths, q, kv)


def later_stage(me, doc_lengths, state, blocks, origin, rows, factor, skip=(0, 0), limit=99, last=False):
    qx, m, la = state
    n, hdim = m.shape
    count = len(blocks)
    held = [pltpu.VMEM((n, hdim), jnp.float32), pltpu.VMEM((n, 2 * hdim), jnp.float32)]
    outs = [pltpu.VMEM((rows, n // rows * hdim), jnp.bfloat16)] if last else []
    result = pl.pallas_call(
        functools.partial(later_kernel, origin, count, skip, limit, last, rows, factor),
        out_shape=outs + held,
        in_specs=[SMEM, SMEM] + [VMEM] * (count + 3),
        out_specs=[VMEM] * (len(outs) + 2),
        input_output_aliases={3 + count + i: len(outs) + i for i in range(2)},
        scratch_shapes=[pltpu.VMEM((count, rows, 2 * hdim), jnp.bfloat16)] * 2,
        compiler_params=pltpu.CompilerParams(vmem_limit_bytes=28 << 20),
        cost_estimate=pl.CostEstimate(
            flops=2_000_000_000 * count, bytes_accessed=300_000 * count, transcendentals=2_000_000 * count
        ),
    )(me, doc_lengths, qx, *blocks, m, la)
    return result[0] if last else (qx, *result)


def on_device(queries, keys, values, doc_lengths):
    rows, group, hdim = queries.shape
    count = lax.axis_size("ctx")
    factor = 1.4426950408889634 / hdim**0.5
    me = lax.axis_index("ctx").reshape(1)
    own = jnp.concatenate([keys[:, 0, :], values[:, 0, :]], axis=1)

    def swap(x, bit):
        return lax.ppermute(x, "ctx", [(i, i ^ bit) for i in range(count)])

    def plane(x):
        return lax.ppermute(x, "ctx", [(i, (i + 4) % count) for i in range(count)])

    z1 = plane(own)
    x0 = swap(own, 2)
    c0 = swap(own, 1)
    q = pltpu.with_memory_space_constraint(queries.reshape(rows * group, hdim), pltpu.HBM)
    state = own_stage(me, doc_lengths, q, own, rows, group, factor)
    z1, x0, c0, state = lax.optimization_barrier((z1, x0, c0, state))
    z2 = plane(z1)
    x1 = swap(z1, 2)
    xc0 = swap(x0, 1)
    c1 = swap(z1, 1)
    near = [c0, x0, xc0, z1, c1]
    state = later_stage(me, doc_lengths, state, near, 1, rows, factor, limit=EARLY)
    z2, x1, state = lax.optimization_barrier((z2, x1, state))
    x2 = swap(z2, 2)
    xc2 = swap(z2, 3)
    xc1 = swap(x1, 1)
    c2 = swap(z2, 1)
    state = later_stage(me, doc_lengths, state, near + [x1, xc1, z2, c2], 1, rows, factor, skip=(EARLY, len(near)))
    x2, xc2, state = lax.optimization_barrier((x2, xc2, state))
    out = later_stage(me, doc_lengths, state, [x2, xc2], 10, rows, factor, last=True)
    return lax.all_to_all(out, "head", split_axis=0, concat_axis=1, tiled=True)


def solution(mesh):
    placed = (P("ctx", "head", None), P("ctx", "head", None), P("ctx", "head", None), P())

    return jax.shard_map(
        on_device, mesh=mesh, in_specs=placed, out_specs=P(("ctx", "head"), None), check_vma=False
    )
```

```python
import functools

import jax
import jax.numpy as jnp
from jax import lax
from jax.experimental import pallas as pl
from jax.experimental.pallas import tpu as pltpu
from jax.sharding import PartitionSpec as P

NEG = -1e30
NT = (((1,), (1,)), ((), ()))
HALF = 256
GROUP = 256
EARLY = 2
VMEM = pl.BlockSpec(memory_space=pltpu.VMEM)
SMEM = pl.BlockSpec(memory_space=pltpu.SMEM)


def first_doc(base, len_ref, visit):
    def doc(d, carry):
        end, low, high = carry
        length = len_ref[d]
        if visit is not None:
            visit(end, length)
        here = (end <= base) & (end + length > base)
        return end + length, jnp.where(here, end, low), jnp.where(here, end + length, high)

    _, low, high = lax.fori_loop(0, len_ref.shape[0], doc, (jnp.int32(0),) * 3, unroll=visit is None)
    return low, high


def own_kernel(rows, group, factor, me_ref, len_ref, q_hbm, kv_ref, qx_ref, m_ref, la_ref, q_s, start_s, sem):
    n, hdim = q_s.shape
    copy = pltpu.make_async_copy(q_hbm, q_s, sem)
    copy.start()
    base = me_ref[0] * rows
    tokens = base + lax.broadcasted_iota(jnp.int32, (rows, hdim), 0)
    start_s[...] = jnp.zeros_like(start_s)

    def visit(start, length):
        @pl.when((start < base + rows) & (start + length > base))
        def _():
            start_s[...] = jnp.where(tokens >= start, start, start_s[...])

    _, high = first_doc(base, len_ref, visit)
    lane = lax.broadcasted_iota(jnp.int32, (1, hdim), 1)
    token = base + lax.broadcasted_iota(jnp.int32, (n, hdim), 0) // group
    flag = (lane == 0) | ((lane == 1) & (token >= high))
    qx_ref[:, hdim : 2 * hdim] = jnp.where(flag, 1.0, 0.0).astype(jnp.bfloat16)
    copy.wait()
    qx_ref[:, 0:hdim] = q_s[...]
    step = 128
    for t in range(0, rows, step):
        keys, many = t + step, step * group
        rs = pl.ds(t * group, many)
        s = lax.dot_general(q_s[rs, :], kv_ref[0:keys, 0:hdim], NT, preferred_element_type=jnp.float32)
        spread = lambda x: jnp.broadcast_to(x[:, None, :], (step, group, hdim)).reshape(many, hdim)
        low = spread(start_s[pl.ds(t, step), :])
        now = spread(base + t + lax.broadcasted_iota(jnp.int32, (step, hdim), 0))
        parts = []
        for j in range(0, keys, hdim):
            pos = base + j + lane
            ok = pos >= low
            if j + hdim > t:
                ok = ok & (pos <= now)
            parts.append(jnp.where(ok, s[:, j : j + hdim], NEG))
        top = jnp.max(functools.reduce(jnp.maximum, parts), axis=1, keepdims=True)
        top = jnp.broadcast_to(top, (many, hdim))
        parts = [jnp.exp2((x - top) * factor) for x in parts]
        total = jnp.sum(functools.reduce(jnp.add, parts), axis=1, keepdims=True)
        weight = jnp.concatenate([x.astype(jnp.bfloat16) for x in parts], axis=1)
        m_ref[rs, :] = top
        la_ref[rs, 0:hdim] = jnp.broadcast_to(total, (many, hdim))
        la_ref[rs, hdim : 2 * hdim] = jnp.dot(
            weight, kv_ref[0:keys, hdim : 2 * hdim], preferred_element_type=jnp.float32
        )


def later_kernel(origin, count, skip, limit, last, rows, factor, me_ref, len_ref, qx_ref, *refs):
    blocks, refs = refs[:count], refs[count + 2 :]
    out_ref = refs[0] if last else None
    m_ref, la_ref, kx, vx = refs[-4:]
    n = qx_ref.shape[0]
    hdim = qx_ref.shape[1] // 2
    me = me_ref[0]
    low, _ = first_doc(me * rows, len_ref, None)
    groups = n // GROUP

    def index_of(code):
        return lax.bitwise_xor(me - 4 * (code >> 2), code & 3)

    def needed(index):
        return (index >= 0) & (index < me) & (index * rows + rows > low)

    lane = lax.broadcasted_iota(jnp.int32, (rows, hdim), 1)
    place = lax.broadcasted_iota(jnp.int32, (rows, hdim), 0)
    for b in range(count):
        index = index_of(jnp.int32(origin + b))

        @pl.when(needed(index))
        def _():
            early = jnp.where(place + index * rows >= low, 0.0, NEG)
            kx[b, :, 0:hdim] = blocks[b][:, 0:hdim]
            kx[b, :, hdim : 2 * hdim] = jnp.where(lane == 0, early, jnp.where(lane == 1, NEG, 0.0)).astype(jnp.bfloat16)
            vx[b, :, 0:hdim] = jnp.ones((rows, hdim), jnp.bfloat16)
            vx[b, :, hdim : 2 * hdim] = blocks[b][:, hdim : 2 * hdim]

    def attend(b, score, mixed, halves):
        steps = groups * len(halves)

        def soften(s, g):
            rs = pl.ds(g * GROUP, GROUP)
            m = m_ref[rs, :]
            s0, s1 = s[:, 0:hdim], s[:, hdim : 2 * hdim]
            top = jnp.max(jnp.maximum(s0, s1), axis=1, keepdims=True)
            new = jnp.maximum(m, jnp.broadcast_to(top, m.shape))
            weight = jnp.concatenate([jnp.exp2((x - new) * factor).astype(jnp.bfloat16) for x in (s0, s1)], axis=1)
            m_ref[rs, :] = new
            return weight, jnp.exp2((m - new) * factor)

        def flush(o, g, scale):
            rs = pl.ds(g * GROUP, GROUP)
            for j in (0, hdim):
                la_ref[rs, j : j + hdim] = la_ref[rs, j : j + hdim] * scale + o[:, j : j + hdim]

        def multiply(acc, lhs, step):
            fresh = step // groups if step % groups == 0 else None
            pltpu.matmul_acc_lhs(acc, lhs, load_staged_rhs=fresh)

        for i, h in enumerate(halves):
            pltpu.matmul_push_rhs(kx[b, h * HALF : (h + 1) * HALF, :], i, 0, transpose=True)
            pltpu.matmul_push_rhs(vx[b, h * HALF : (h + 1) * HALF, :], i, 1)
        done = []
        for t in range(-1, steps + 2):
            if t + 1 < steps:
                multiply(score[(t + 1) % 2], qx_ref[pl.ds((t + 1) % groups * GROUP, GROUP), :], t + 1)
            if 0 <= t < steps:
                done.append(soften(pltpu.matmul_pop(score[t % 2]), t % groups))
            if 1 <= t < steps + 1:
                multiply(mixed[(t - 1) % 2], done[t - 1][0], t - 1)
            if 2 <= t:
                flush(pltpu.matmul_pop(mixed[(t - 2) % 2]), (t - 2) % groups, done[t - 2][1])

    def run(s0, s1, p0, p1):
        def one(b, rank):
            index = index_of(origin + b)
            need = needed(index)
            take = need & (rank < limit) & ((rank >= skip[0]) | (b >= skip[1]))
            late = index * rows + HALF <= low

            @pl.when(take & jnp.logical_not(late))
            def _():
                attend(b, (s0, s1), (p0, p1), (0, 1))

            @pl.when(take & late)
            def _():
                attend(b, (s0, s1), (p0, p1), (1,))

            return rank + need.astype(jnp.int32)

        lax.fori_loop(0, count, one, jnp.int32(0))

    score = pltpu.ACC(mxu_id=0)((GROUP, 2 * hdim), jnp.float32)
    mixed = pltpu.ACC(mxu_id=1)((GROUP, 2 * hdim), jnp.float32)
    pl.run_scoped(run, score, score, mixed, mixed)
    if last:
        group = n // rows
        m_ref[...] = la_ref[:, hdim : 2 * hdim] / la_ref[:, 0:hdim]
        for h in range(group):
            rs = pl.ds(h, rows, stride=group)
            out_ref[:, h * hdim : (h + 1) * hdim] = m_ref[rs, :].astype(out_ref.dtype)


def own_stage(me, doc_lengths, q, kv, rows, group, factor):
    n, hdim = q.shape
    return pl.pallas_call(
        functools.partial(own_kernel, rows, group, factor),
        out_shape=[
            pltpu.VMEM((n, 2 * hdim), jnp.bfloat16),
            pltpu.VMEM((n, hdim), jnp.float32),
            pltpu.VMEM((n, 2 * hdim), jnp.float32),
        ],
        in_specs=[SMEM, SMEM, pl.BlockSpec(memory_space=pltpu.HBM), VMEM],
        out_specs=[VMEM] * 3,
        scratch_shapes=[
            pltpu.VMEM((n, hdim), jnp.bfloat16),
            pltpu.VMEM((rows, hdim), jnp.int32),
            pltpu.SemaphoreType.DMA(()),
        ],
        compiler_params=pltpu.CompilerParams(vmem_limit_bytes=28 << 20),
        cost_estimate=pl.CostEstimate(flops=1_500_000_000, bytes_accessed=1_500_000, transcendentals=1_500_000),
    )(me, doc_lengths, q, kv)


def later_stage(me, doc_lengths, state, blocks, origin, rows, factor, skip=(0, 0), limit=99, last=False):
    qx, m, la = state
    n, hdim = m.shape
    count = len(blocks)
    held = [pltpu.VMEM((n, hdim), jnp.float32), pltpu.VMEM((n, 2 * hdim), jnp.float32)]
    outs = [pltpu.VMEM((rows, n // rows * hdim), jnp.bfloat16)] if last else []
    result = pl.pallas_call(
        functools.partial(later_kernel, origin, count, skip, limit, last, rows, factor),
        out_shape=outs + held,
        in_specs=[SMEM, SMEM] + [VMEM] * (count + 3),
        out_specs=[VMEM] * (len(outs) + 2),
        input_output_aliases={3 + count + i: len(outs) + i for i in range(2)},
        scratch_shapes=[pltpu.VMEM((count, rows, 2 * hdim), jnp.bfloat16)] * 2,
        compiler_params=pltpu.CompilerParams(vmem_limit_bytes=28 << 20),
        cost_estimate=pl.CostEstimate(
            flops=2_000_000_000 * count, bytes_accessed=300_000 * count, transcendentals=2_000_000 * count
        ),
    )(me, doc_lengths, qx, *blocks, m, la)
    return result[0] if last else (qx, *result)


def on_device(queries, keys, values, doc_lengths):
    rows, group, hdim = queries.shape
    count = lax.axis_size("ctx")
    factor = 1.4426950408889634 / hdim**0.5
    me = lax.axis_index("ctx").reshape(1)
    own = jnp.concatenate([keys[:, 0, :], values[:, 0, :]], axis=1)

    def swap(x, bit):
        return lax.ppermute(x, "ctx", [(i, i ^ bit) for i in range(count)])

    def plane(x):
        return lax.ppermute(x, "ctx", [(i, (i + 4) % count) for i in range(count)])

    z1 = plane(own)
    x0 = swap(own, 2)
    c0 = swap(own, 1)
    q = pltpu.with_memory_space_constraint(queries.reshape(rows * group, hdim), pltpu.HBM)
    state = own_stage(me, doc_lengths, q, own, rows, group, factor)
    z1, x0, c0, state = lax.optimization_barrier((z1, x0, c0, state))
    z2 = plane(z1)
    x1 = swap(z1, 2)
    xc0 = swap(x0, 1)
    c1 = swap(z1, 1)
    near = [c0, x0, xc0, z1, c1]
    state = later_stage(me, doc_lengths, state, near, 1, rows, factor, limit=EARLY)
    z2, x1, state = lax.optimization_barrier((z2, x1, state))
    x2 = swap(z2, 2)
    xc2 = swap(z2, 3)
    xc1 = swap(x1, 1)
    c2 = swap(z2, 1)
    state = later_stage(me, doc_lengths, state, near + [x1, xc1, z2, c2], 1, rows, factor, skip=(EARLY, len(near)))
    x2, xc2, state = lax.optimization_barrier((x2, xc2, state))
    out = later_stage(me, doc_lengths, state, [x2, xc2], 10, rows, factor, last=True)
    return lax.all_to_all(out, "head", split_axis=0, concat_axis=1, tiled=True)


def solution(mesh):
    placed = (P("ctx", "head", None), P("ctx", "head", None), P("ctx", "head", None), P())

    return jax.shard_map(
        on_device, mesh=mesh, in_specs=placed, out_specs=P(("ctx", "head"), None), check_vma=False
    )
```
